512 devices in a mesh: row: 128 (over x, z_hi, y, core), col: 4 (over z_lo).
Axes of the slice: x: 4, y: 4, z: 16 (z_hi: 4, z_lo: 4; z = z_hi * 4 + z_lo), core: 2. Of those that a mesh axis runs over, the one named last changes fastest.
Arguments:
- state: bfloat16 [4, 512, 512, 128], P('col', 'row'), may hold values from -6 to 6
- accum: float32 [4, 512, 512, 128], P('col', 'row'), may hold values from -6 to 6
- poisson_weight: float32 [1], replicated, may hold values from 0.2 to 1
- route1_blocks: bfloat16 [2, 8, 4, 64, 64], replicated, may hold values from -0.25 to 0.25
- route1_cols: int32 [2, 8, 4], replicated, may hold values from 0 to 7, as said below
- route2_blocks: bfloat16 [5, 8, 4, 64, 64], replicated, may hold values from -0.25 to 0.25
- route2_cols: int32 [5, 8, 4], replicated, may hold values from 0 to 7, as said below
- route3_factors: bfloat16 [2, 128, 128], replicated, may hold values from -0.375 to 0.375
- fleet_offsets: int32 [3], replicated, may hold values from -1 to 1, as said below
Outputs:
- next_state: bfloat16 [4, 512, 512, 128], P('col', 'row')
- next_accum: float32 [4, 512, 512, 128], P('col', 'row')
The draws below stay inside these ranges and needn't reach their ends.
Inputs may be any that keep to these rules, and one draw needn't show every extreme that they name: `route1_cols`: within each block row of each factor the 4 block columns are distinct. `route2_cols`: within each block row of each factor the 4 block columns are distinct. `fleet_offsets`: both -1 and +1 occur among the offsets.
All inputs are finite; a program needn't handle non-finite values.
Results may differ from the reference program's by a relative error of at most 0.0025.
Values may be sent and summed in bfloat16 or wider, within the bound.
No kernel may reach another device: no remote copies, remote signals or barrier semaphores. Data moves between devices by JAX's collectives and lax.ppermute only.
A program may use at most 64 MiB of HBM per device.

```python
import math
import jax
import jax.numpy as jnp
from jax import lax

ROUTE = 512
BLOCK = 64
NNZ = 4
W3 = 128
FLEET = 4
KTERMS = 3
NB = 8


def block_columns(key, factors):
    count = ROUTE // BLOCK
    keys = jax.random.split(key, factors * count)
    perms = jax.vmap(lambda single: jax.random.permutation(single, count))(keys)[:, :NNZ]
    return perms.reshape(factors, count, NNZ).astype(jnp.int32)


def draw_route1_cols(key, part):
    return block_columns(jax.random.fold_in(key, 11), 2)


def draw_route2_cols(key, part):
    return block_columns(jax.random.fold_in(key, 23), 2 + KTERMS)


def draw_fleet_offsets(key, part):
    first_key, second_key = jax.random.split(jax.random.fold_in(key, 37))
    pair = jax.random.permutation(first_key, 2).astype(jnp.int32) * 2 - 1
    others = jax.random.randint(second_key, (KTERMS - 2,), -1, 2).astype(jnp.int32)
    return jnp.concatenate([pair, others]).astype(jnp.int32)


def shard_levels(rng, dims, pieces, least, largest):
    def one(axis_at, parts):
        steps = jax.random.uniform(jax.random.fold_in(jax.random.fold_in(rng, 6), axis_at), (parts,), jnp.float32, least / len(pieces), largest / len(pieces))
        return jnp.repeat(jnp.exp(steps), dims[axis_at] // parts).reshape((-1,) + (1,) * (len(dims) - axis_at - 1))

    gain = one(*pieces[0])
    for cut in pieces[1:]:
        gain = gain * one(*cut)
    return gain


def normal_values(stream_key, shape, scale, bound, cuts=(), kind=jnp.bfloat16):
    gain = shard_levels(stream_key, shape, cuts, -0.22, 0.18) if cuts else 1.0
    entries = jax.random.normal(stream_key, shape, jnp.float32) * scale * gain
    return jnp.minimum(jnp.maximum(entries, -bound), bound).astype(kind)


def setup_inputs(seed: int = 0) -> dict:
    splits = jax.random.split(jax.random.key(seed), 10)
    state = normal_values(splits[0], (FLEET, ROUTE, ROUTE, W3), 1.0, 6.0, ((0, 4), (1, 128)))
    accum = normal_values(splits[1], (FLEET, ROUTE, ROUTE, W3), 1.0, 6.0, ((0, 4), (1, 128)), jnp.float32)
    poisson_weight = jnp.clip(jnp.exp(jax.random.uniform(splits[2], (1,), jnp.float32, math.log(0.2), math.log(1.0))), 0.2, 1.0)
    route1_blocks = normal_values(splits[3], (2, NB, NNZ, BLOCK, BLOCK), (2 * NNZ * BLOCK) ** -0.5, 0.25)
    route1_cols = draw_route1_cols(jax.random.fold_in(splits[9], 71), 0)
    route2_blocks = normal_values(splits[5], (2 + KTERMS, NB, NNZ, BLOCK, BLOCK), (2 * NNZ * BLOCK) ** -0.5, 0.25)
    route2_cols = draw_route2_cols(jax.random.fold_in(splits[9], 71), 0)
    route3_factors = normal_values(splits[7], (2, W3, W3), (2 * W3) ** -0.5, 0.375)
    fleet_offsets = draw_fleet_offsets(jax.random.fold_in(splits[9], 71), 0)
    return dict(state=state, accum=accum, poisson_weight=poisson_weight, route1_blocks=route1_blocks, route1_cols=route1_cols, route2_blocks=route2_blocks, route2_cols=route2_cols, route3_factors=route3_factors, fleet_offsets=fleet_offsets)


def densify(blocks, columns):
    count = blocks.shape[0]
    width = blocks.shape[2]
    onehot = (columns[:, :, None] == jnp.arange(count, dtype=jnp.int32)[None, None, :]).astype(jnp.float32)
    dense = jnp.einsum("rkij,rkc->ricj", blocks.astype(jnp.float32), onehot)
    return dense.reshape(count * width, count * width)


def along_first(matrix, field):
    return jnp.einsum("ab,fbmc->famc", matrix.astype(jnp.float32), field.astype(jnp.float32))


def along_second(matrix, field):
    return jnp.einsum("mn,fanc->famc", matrix.astype(jnp.float32), field.astype(jnp.float32))


def along_third(matrix, field):
    return jnp.einsum("cd,famd->famc", matrix.astype(jnp.float32), field.astype(jnp.float32))


def reference(state, accum, poisson_weight, route1_blocks, route1_cols, route2_blocks, route2_cols, route3_factors, fleet_offsets):
    field = state.astype(jnp.float32)
    first_local = densify(route1_blocks[0], route1_cols[0])
    first_sync = densify(route1_blocks[1], route1_cols[1])
    second_all = [densify(route2_blocks[term], route2_cols[term]) for term in range(2 + KTERMS)]
    sectioned = along_third(route3_factors[1], field).astype(jnp.bfloat16)
    coupled = along_second(second_all[1], sectioned).astype(jnp.bfloat16)
    total = field + along_first(first_local, field) + along_first(first_sync, coupled)
    total = total + along_second(second_all[0], field) + along_third(route3_factors[0], field)
    for term_index in range(KTERMS):
        moved = along_second(second_all[2 + term_index], field)
        padded = jnp.pad(moved, ((1, 1), (0, 0), (0, 0), (0, 0)))
        start = (1 - fleet_offsets[term_index]).astype(jnp.int32)
        total = total + lax.dynamic_slice_in_dim(padded, start, FLEET, 0)
    return total.astype(jnp.bfloat16), accum + poisson_weight[0] * total
```

```python
import jax
import jax.numpy as jnp
from jax import lax
from jax.experimental import pallas as pl
from jax.experimental.pallas import tpu as pltpu
from jax.sharding import PartitionSpec as P

NX, NZ, NY, NC = 4, 4, 4, 2
PLANE = NX * NY * NC
BF = jnp.bfloat16
F32 = jnp.float32


def row_of(x, z, y, core):
    return ((x * NZ + z % NZ) * NY + y) * NC + core


def plane_groups():
    return [
        [row_of(x, z, y, c) for x in range(NX) for y in range(NY) for c in range(NC)]
        for z in range(NZ)
    ]


def z_shift(step):
    return [
        (row_of(x, z, y, c), row_of(x, z + step, y, c))
        for x in range(NX)
        for z in range(NZ)
        for y in range(NY)
        for c in range(NC)
    ]


def cost(flops, moved):
    return pl.CostEstimate(flops=flops, bytes_accessed=moved, transcendentals=0)


SMALL = pltpu.CompilerParams(vmem_limit_bytes=24 * 1024 * 1024)


def iota2(shape):
    return (
        lax.broadcasted_iota(jnp.int32, shape, 0),
        lax.broadcasted_iota(jnp.int32, shape, 1),
    )


def onehot(rows_match):
    return jnp.where(rows_match, 1.0, 0.0).astype(BF)


def dot(a, b):
    return jnp.dot(a, b, preferred_element_type=F32)


def factors_kernel(cols1, cols2, own, b1, b2, second, sync2, first, dense):
    second[...] = jnp.zeros_like(second)
    sync2[...] = jnp.zeros_like(sync2)
    dense[...] = jnp.zeros_like(dense)

    def place(dst, r, base, c, blk):
        zero = jnp.zeros_like(blk)
        left = jnp.concatenate([blk, zero], axis=1)
        right = jnp.concatenate([zero, blk], axis=1)
        wide = jnp.where((c & 1) == 0, left, right)
        at = (
            pl.ds(pl.multiple_of(r * 64, 64), 64),
            pl.ds(pl.multiple_of(base + (c >> 1) * 128, 128), 128),
        )
        dst[at] = dst[at] + wide

    def row(r, carry):
        for k in range(4):
            for t in range(2):
                place(dense.at[t], r, 0, cols1[t * 32 + r * 4 + k], b1[t, r, k])
            place(sync2, r, 0, cols2[32 + r * 4 + k], b2[1, r, k])
            for t, base in ((0, 0), (2, 512), (3, 1024), (4, 1536)):
                place(second, r, base, cols2[t * 32 + r * 4 + k], b2[t, r, k])
        return carry

    lax.fori_loop(0, 8, row, 0)
    me = own[0]
    i, j = iota2((512, 512))
    source = ((j >> 5) & 3) * 128 + (j >> 7) * 32 + (j & 31)
    swap = onehot(i == source)
    for t in range(2):
        rows = jnp.concatenate(
            [dense[t, pl.ds(pl.multiple_of(x * 128 + me * 32, 32), 32), :] for x in range(4)],
            axis=0,
        )
        turned = dot(rows, swap).astype(BF)
        for z in range(4):
            slot = (z - me + 4) & 3
            first[t, slot] = turned[:, z * 128 : (z + 1) * 128]


def factors(cols1, cols2, own, b1, b2):
    smem = pl.BlockSpec(memory_space=pltpu.SMEM)
    vmem = pl.BlockSpec(memory_space=pltpu.VMEM)
    return pl.pallas_call(
        factors_kernel,
        out_shape=(
            jax.ShapeDtypeStruct((512, 2048), BF),
            jax.ShapeDtypeStruct((512, 512), BF),
            jax.ShapeDtypeStruct((2, 4, 128, 128), BF),
        ),
        in_specs=[smem, smem, smem, vmem, vmem],
        out_specs=(vmem, vmem, vmem),
        scratch_shapes=[pltpu.VMEM((2, 512, 512), BF)],
        cost_estimate=cost(300_000_000, 8_000_000),
        compiler_params=SMALL,
        name="factors",
    )(cols1, cols2, own, b1, b2)


def arrange_kernel(got, half_a, half_b):
    i, j = iota2((256, 256))
    move = onehot(j == ((i >> 2) & 3) * 64 + (i & 3) * 16 + (i >> 4))
    for g in range(8):
        block = got[4 * g : 4 * g + 4].reshape(256, 128)
        out = dot(move, block).astype(BF)
        for m in range(16):
            dst = half_a if m < 8 else half_b
            dst[m % 8, g * 16 : g * 16 + 16, :] = out[m * 16 : m * 16 + 16, :]


def arrange(got):
    half = jax.ShapeDtypeStruct((8, 128, 128), BF)
    return pl.pallas_call(
        arrange_kernel,
        out_shape=(half, half),
        cost_estimate=cost(130_000_000, 1_100_000),
        compiler_params=SMALL,
        name="arrange",
    )(got)


def pair_products(first, s3_twice, slot, half, p, add1, add2):
    x = jnp.concatenate([half[2 * p], half[2 * p + 1]], axis=1)
    section = dot(x, s3_twice).astype(BF)
    one = dot(first[0, slot], x)
    two = dot(first[1, slot], section)
    if add1 is not None:
        one, two = one + add1, two + add2
    return one, two


def twice(s3):
    zero = jnp.zeros_like(s3)
    return jnp.concatenate(
        [jnp.concatenate([s3, zero], axis=1), jnp.concatenate([zero, s3], axis=1)], axis=0
    )


def near_kernel(first, s3, a0, b0, a3, b3, a1, b1, acc):
    s3_twice = twice(s3[...])
    for h, halves in enumerate(((a0, a3, a1), (b0, b3, b1))):
        for p in range(4):
            one, two = None, None
            for slot, half in zip((0, 3, 1), halves):
                one, two = pair_products(first, s3_twice, slot, half, p, one, two)
            at = (h * 4 + p) * 256
            acc[0, :, at : at + 256] = one
            acc[1, :, at : at + 256] = two


def near(first, s3, pieces):
    return pl.pallas_call(
        near_kernel,
        out_shape=jax.ShapeDtypeStruct((2, 128, 2048), F32),
        cost_estimate=cost(800_000_000, 4_000_000),
        compiler_params=SMALL,
        name="near",
    )(first, s3, *pieces)


def far_kernel(first, s3, acc, a2, b2, out, keep):
    s3_twice = twice(s3[...])
    for h, half in enumerate((a2, b2)):
        for p in range(4):
            at = (h * 4 + p) * 256
            one, two = pair_products(
                first, s3_twice, 2, half, p, acc[0, :, at : at + 256], acc[1, :, at : at + 256]
            )
            keep[0, :, at : at + 256] = one.astype(BF)
            keep[1, :, at : at + 256] = two.astype(BF)
    i, j = iota2((256, 256))
    move = onehot(i == ((j >> 2) & 3) * 64 + (j & 3) * 16 + (j >> 4))
    for t in range(2):
        for g in range(8):
            rows = jnp.concatenate(
                [keep[t, g * 16 : g * 16 + 16, m * 128 : m * 128 + 128] for m in range(16)],
                axis=0,
            )
            out[4 * g : 4 * g + 4, t] = dot(move, rows).astype(BF).reshape(4, 64, 128)


def far(first, s3, acc, a2, b2):
    return pl.pallas_call(
        far_kernel,
        out_shape=jax.ShapeDtypeStruct((32, 2, 64, 128), BF),
        scratch_shapes=[pltpu.VMEM((2, 128, 2048), BF)],
        cost_estimate=cost(400_000_000, 4_000_000),
        compiler_params=SMALL,
        name="far",
    )(first, s3, acc, a2, b2)


def local_kernel(offsets, second, r3, state, before, after, out, stack):
    x = state[0]
    stack[0:512, :] = x
    for k in range(3):
        off = offsets[k]
        rows = slice(512 * (k + 1), 512 * (k + 2))

        @pl.when(off == 1)
        def _():
            stack[rows, :] = before[0]

        @pl.when(off == 0)
        def _():
            stack[rows, :] = state[0]

        @pl.when(off == -1)
        def _():
            stack[rows, :] = after[0]

    out[0] = x.astype(F32) + dot(x, r3[...]) + dot(second[...], stack[...])


def local_terms(offsets, second, r3, state, before, after):
    slab = pl.BlockSpec((1, 512, 128), lambda b: (b, 0, 0))
    return pl.pallas_call(
        local_kernel,
        grid=(4,),
        out_shape=jax.ShapeDtypeStruct((4, 512, 128), F32),
        in_specs=[
            pl.BlockSpec(memory_space=pltpu.SMEM),
            pl.BlockSpec((512, 2048), lambda b: (0, 0)),
            pl.BlockSpec((128, 128), lambda b: (0, 0)),
            slab,
            slab,
            slab,
        ],
        out_specs=slab,
        scratch_shapes=[pltpu.VMEM((2048, 128), BF)],
        cost_estimate=cost(1_200_000_000, 5_000_000),
        compiler_params=SMALL,
        name="local_terms",
    )(offsets, second, r3, state, before, after)


def finish_kernel(weight, sync2, back, base, accum, state_out, accum_out):
    one = back[:, 0, 0].reshape(512, 128)
    two = back[:, 1, 0].reshape(512, 128)
    total = base[0] + one.astype(F32) + dot(sync2[...], two)
    state_out[0] = total.astype(BF)
    accum_out[0] = accum[0] + weight[0] * total


def finish(weight, sync2, back, base, accum):
    slab = pl.BlockSpec((1, 512, 128), lambda b: (b, 0, 0))
    return pl.pallas_call(
        finish_kernel,
        grid=(4,),
        out_shape=(
            jax.ShapeDtypeStruct((4, 512, 128), BF),
            jax.ShapeDtypeStruct((4, 512, 128), F32),
        ),
        in_specs=[
            pl.BlockSpec(memory_space=pltpu.SMEM),
            pl.BlockSpec((512, 512), lambda b: (0, 0)),
            pl.BlockSpec((32, 2, 1, 16, 128), lambda b: (0, 0, b, 0, 0)),
            slab,
            slab,
        ],
        out_specs=(slab, slab),
        cost_estimate=cost(300_000_000, 6_000_000),
        compiler_params=SMALL,
        name="finish",
    )(weight, sync2, back, base, accum)


def local(
    state,
    accum,
    poisson_weight,
    route1_blocks,
    route1_cols,
    route2_blocks,
    route2_cols,
    route3_factors,
    fleet_offsets,
):
    field = state[0]
    levels = lax.axis_size("col")
    up = [(i, i + 1) for i in range(levels - 1)]
    down = [(i + 1, i) for i in range(levels - 1)]
    before = lax.ppermute(field, "col", up)
    after = lax.ppermute(field, "col", down)
    groups = plane_groups()

    split = field.reshape(4, PLANE, 16, 128).transpose(1, 0, 2, 3).reshape(PLANE, 64, 128)
    got = lax.all_to_all(split, "row", 0, 0, tiled=True, axis_index_groups=groups)
    got, before, after = lax.optimization_barrier((got, before, after))
    a0, b0 = arrange(got)

    plus, minus = z_shift(1), z_shift(-1)
    a3 = lax.ppermute(a0, "row", plus)
    b1 = lax.ppermute(b0, "row", minus)
    b3 = lax.ppermute(b0, "row", plus)
    a1 = lax.ppermute(a0, "row", minus)
    a2 = lax.ppermute(a3, "row", plus)
    b2 = lax.ppermute(b1, "row", minus)

    own = (lax.axis_index("row") // (NY * NC)) % NZ
    second, sync2, first = factors(
        route1_cols.reshape(-1),
        route2_cols.reshape(-1),
        own.astype(jnp.int32).reshape(1),
        route1_blocks,
        route2_blocks,
    )
    turned = jnp.swapaxes(route3_factors, 1, 2)
    base = local_terms(fleet_offsets, second, turned[0], field, before, after)
    acc = near(first, turned[1], (a0, b0, a3, b3, a1, b1))
    sent = far(first, turned[1], acc, a2, b2)
    back = lax.all_to_all(
        sent.reshape(PLANE, 128, 128), "row", 0, 0, tiled=True, axis_index_groups=groups
    ).reshape(PLANE, 2, 4, 16, 128)
    state_out, accum_out = finish(poisson_weight, sync2, back, base, accum[0])
    return state_out[None], accum_out[None]


def solution(mesh):
    placed = (
        P("col", "row", None, None),
        P("col", "row", None, None),
        P(),
        P(),
        P(),
        P(),
        P(),
        P(),
        P(),
    )
    return jax.shard_map(
        local,
        mesh=mesh,
        in_specs=placed,
        out_specs=(P("col", "row", None, None), P("col", "row", None, None)),
        check_vma=False,
    )
```

```python
import functools

import jax
import jax.numpy as jnp
from jax import lax
from jax.experimental import pallas as pl
from jax.experimental.pallas import tpu as pltpu
from jax.sharding import PartitionSpec as P

NX, NZ, NY, NC = 4, 4, 4, 2
PLANE = NX * NY * NC
BF = jnp.bfloat16
F32 = jnp.float32


def row_of(x, z, y, core):
    return ((x * NZ + z % NZ) * NY + y) * NC + core


def plane_groups():
    return [
        [row_of(x, z, y, c) for x in range(NX) for y in range(NY) for c in range(NC)]
        for z in range(NZ)
    ]


def z_swap(sign):
    return [
        (row_of(x, z, y, c), row_of(x, z + (sign if (z + c) % 2 == 0 else -sign), y, c))
        for x in range(NX)
        for z in range(NZ)
        for y in range(NY)
        for c in range(NC)
    ]


def place_of(row):
    z, core = (row >> 3) & 3, row & 1
    step = 1 - 2 * ((z + core) & 1)
    return z, step, half_of(z, core)


def half_of(z, core):
    return ((z + 1 - core) >> 1) & 1


def cost(flops, moved):
    return pl.CostEstimate(flops=flops, bytes_accessed=moved, transcendentals=0)


SMALL = pltpu.CompilerParams(vmem_limit_bytes=24 * 1024 * 1024)


def iota2(shape):
    return (
        lax.broadcasted_iota(jnp.int32, shape, 0),
        lax.broadcasted_iota(jnp.int32, shape, 1),
    )


def onehot(rows_match):
    return jnp.where(rows_match, 1.0, 0.0).astype(BF)


def dot(a, b):
    return jnp.dot(a, b, preferred_element_type=F32)


def factors_kernel(cols1, cols2, row_ref, b1, b2, second, sync2, first, dense):
    second[...] = jnp.zeros_like(second)
    sync2[...] = jnp.zeros_like(sync2)
    dense[...] = jnp.zeros_like(dense)

    def place(dst, r, base, c, blk):
        zero = jnp.zeros_like(blk)
        left = jnp.concatenate([blk, zero], axis=1)
        right = jnp.concatenate([zero, blk], axis=1)
        wide = jnp.where((c & 1) == 0, left, right)
        at = (
            pl.ds(pl.multiple_of(r * 64, 64), 64),
            pl.ds(pl.multiple_of(base + (c >> 1) * 128, 128), 128),
        )
        dst[at] = dst[at] + wide

    def row(r, carry):
        for k in range(4):
            for t in range(2):
                place(dense.at[t], r, 0, cols1[t * 32 + r * 4 + k], b1[t, r, k])
            place(sync2, r, 0, cols2[32 + r * 4 + k], b2[1, r, k])
            for t, base in ((0, 0), (2, 512), (3, 1024), (4, 1536)):
                place(second, r, base, cols2[t * 32 + r * 4 + k], b2[t, r, k])
        return carry

    lax.fori_loop(0, 8, row, 0)
    me, step, _ = place_of(row_ref[0])
    i, j = iota2((512, 512))
    source = ((j >> 5) & 3) * 128 + (j >> 7) * 32 + (j & 31)
    swap = onehot(i == source)
    for d in range(2):
        at = (me + d * step) & 3
        for t in range(2):
            rows = jnp.concatenate(
                [dense[t, pl.ds(pl.multiple_of(x * 128 + at * 32, 32), 32), :] for x in range(4)],
                axis=0,
            )
            turned = dot(rows, swap).astype(BF)
            for z in range(4):
                first[d, t, ((z - me) * step) & 3] = turned[:, z * 128 : (z + 1) * 128]


def factors(cols1, cols2, row, b1, b2):
    smem = pl.BlockSpec(memory_space=pltpu.SMEM)
    vmem = pl.BlockSpec(memory_space=pltpu.VMEM)
    return pl.pallas_call(
        factors_kernel,
        out_shape=(
            jax.ShapeDtypeStruct((512, 2048), BF),
            jax.ShapeDtypeStruct((512, 512), BF),
            jax.ShapeDtypeStruct((2, 2, 4, 128, 128), BF),
        ),
        in_specs=[smem, smem, smem, vmem, vmem],
        out_specs=(vmem, vmem, vmem),
        scratch_shapes=[pltpu.VMEM((2, 512, 512), BF)],
        cost_estimate=cost(300_000_000, 8_000_000),
        compiler_params=SMALL,
        name="factors",
    )(cols1, cols2, row, b1, b2)


def arrange_kernel(row_ref, got, mine, other):
    _, _, half = place_of(row_ref[0])
    i, j = iota2((256, 256))
    move = onehot(j == ((i >> 2) & 3) * 64 + (i & 3) * 16 + (i >> 4))
    for g in range(8):
        block = got[4 * g : 4 * g + 4].reshape(256, 128)
        out = dot(move, block)
        at = slice(g * 16, g * 16 + 16)
        for m in range(8):
            low = out[m * 16 : m * 16 + 16, :]
            high = out[m * 16 + 128 : m * 16 + 144, :]
            mine[m, at, :] = jnp.where(half == 0, low, high).astype(BF)
            other[m, at, :] = jnp.where(half == 0, high, low).astype(BF)


def arrange(row, got):
    one = jax.ShapeDtypeStruct((8, 128, 128), BF)
    return pl.pallas_call(
        arrange_kernel,
        out_shape=(one, one),
        in_specs=[pl.BlockSpec(memory_space=pltpu.SMEM), pl.BlockSpec(memory_space=pltpu.VMEM)],
        cost_estimate=cost(130_000_000, 1_100_000),
        compiler_params=SMALL,
        name="arrange",
    )(row, got)


def twice(s3):
    zero = jnp.zeros_like(s3)
    return jnp.concatenate(
        [jnp.concatenate([s3, zero], axis=1), jnp.concatenate([zero, s3], axis=1)], axis=0
    )


def near_kernel(first, s3, mine, pair, cross, acc):
    s3_twice = twice(s3[...])
    for p in range(4):
        sums = [[None, None], [None, None]]
        for slot, part in ((0, mine), (1, pair), (3, cross)):
            x = jnp.concatenate([part[2 * p], part[2 * p + 1]], axis=1)
            inputs = (x, dot(x, s3_twice).astype(BF))
            for d in range(2):
                for t in range(2):
                    got = dot(first[d, t, slot], inputs[t])
                    sums[d][t] = got if sums[d][t] is None else sums[d][t] + got
        for d in range(2):
            for t in range(2):
                acc[d, t, :, p * 256 : p * 256 + 256] = sums[d][t]


def near(first, s3, mine, pair, cross):
    return pl.pallas_call(
        near_kernel,
        out_shape=jax.ShapeDtypeStruct((2, 2, 128, 1024), F32),
        cost_estimate=cost(700_000_000, 4_000_000),
        compiler_params=SMALL,
        name="near",
    )(first, s3, mine, pair, cross)


def far_kernel(d, first, s3, acc, part, out, keep):
    s3_twice = twice(s3[...])
    for p in range(4):
        at = slice(p * 256, p * 256 + 256)
        x = jnp.concatenate([part[2 * p], part[2 * p + 1]], axis=1)
        inputs = (x, dot(x, s3_twice).astype(BF))
        for t in range(2):
            keep[t, :, at] = (acc[d, t, :, at] + dot(first[d, t, 2], inputs[t])).astype(BF)
    i, j = iota2((128, 128))
    move = onehot(i == ((j >> 2) & 3) * 32 + (j & 3) * 8 + (j >> 4))
    for t in range(2):
        for g in range(8):
            rows = jnp.concatenate(
                [keep[t, g * 16 : g * 16 + 16, m * 128 : m * 128 + 128] for m in range(8)],
                axis=0,
            )
            out[4 * g : 4 * g + 4, t] = dot(move, rows).astype(BF).reshape(4, 32, 128)


def far(d, first, s3, acc, part):
    return pl.pallas_call(
        functools.partial(far_kernel, d),
        out_shape=jax.ShapeDtypeStruct((32, 2, 32, 128), BF),
        scratch_shapes=[pltpu.VMEM((2, 128, 1024), BF)],
        cost_estimate=cost(200_000_000, 2_000_000),
        compiler_params=SMALL,
        name="far",
    )(first, s3, acc, part)


def local_kernel(offsets, second, r3, state, before, after, out, stack):
    x = state[0]
    stack[0:512, :] = x
    for k in range(3):
        off = offsets[k]
        rows = slice(512 * (k + 1), 512 * (k + 2))

        @pl.when(off == 1)
        def _():
            stack[rows, :] = before[0]

        @pl.when(off == 0)
        def _():
            stack[rows, :] = state[0]

        @pl.when(off == -1)
        def _():
            stack[rows, :] = after[0]

    out[0] = x.astype(F32) + dot(x, r3[...]) + dot(second[...], stack[...])


def local_terms(offsets, second, r3, state, before, after):
    slab = pl.BlockSpec((1, 512, 128), lambda b: (b, 0, 0))
    return pl.pallas_call(
        local_kernel,
        grid=(4,),
        out_shape=jax.ShapeDtypeStruct((4, 512, 128), F32),
        in_specs=[
            pl.BlockSpec(memory_space=pltpu.SMEM),
            pl.BlockSpec((512, 2048), lambda b: (0, 0)),
            pl.BlockSpec((128, 128), lambda b: (0, 0)),
            slab,
            slab,
            slab,
        ],
        out_specs=slab,
        scratch_shapes=[pltpu.VMEM((2048, 128), BF)],
        cost_estimate=cost(1_200_000_000, 5_000_000),
        compiler_params=SMALL,
        name="local_terms",
    )(offsets, second, r3, state, before, after)


def finish_kernel(weight, row_ref, sync2, back1, back2, base, accum, state_out, accum_out):
    z, _, _ = place_of(row_ref[0])
    core = lax.broadcasted_iota(jnp.int32, (PLANE, 8, 128), 0) & 1
    low_first = jnp.where(core == 0, half_of(z, 0), half_of(z, 1)) == 0

    def joined(t):
        one, two = back1[:, t, 0].astype(F32), back2[:, t, 0].astype(F32)
        parts = [jnp.where(low_first, one, two), jnp.where(low_first, two, one)]
        return jnp.concatenate(parts, axis=1).reshape(512, 128)

    total = base[0] + joined(0) + dot(sync2[...], joined(1).astype(BF))
    state_out[0] = total.astype(BF)
    accum_out[0] = accum[0] + weight[0] * total


def finish(weight, row, sync2, back1, back2, base, accum):
    slab = pl.BlockSpec((1, 512, 128), lambda b: (b, 0, 0))
    part = pl.BlockSpec((32, 2, 1, 8, 128), lambda b: (0, 0, b, 0, 0))
    smem = pl.BlockSpec(memory_space=pltpu.SMEM)
    return pl.pallas_call(
        finish_kernel,
        grid=(4,),
        out_shape=(
            jax.ShapeDtypeStruct((4, 512, 128), BF),
            jax.ShapeDtypeStruct((4, 512, 128), F32),
        ),
        in_specs=[smem, smem, pl.BlockSpec((512, 512), lambda b: (0, 0)), part, part, slab, slab],
        out_specs=(slab, slab),
        cost_estimate=cost(300_000_000, 6_000_000),
        compiler_params=SMALL,
        name="finish",
    )(weight, row, sync2, back1, back2, base, accum)


def local(
    state,
    accum,
    poisson_weight,
    route1_blocks,
    route1_cols,
    route2_blocks,
    route2_cols,
    route3_factors,
    fleet_offsets,
):
    field = state[0]
    levels = lax.axis_size("col")
    up = [(i, i + 1) for i in range(levels - 1)]
    down = [(i + 1, i) for i in range(levels - 1)]
    before = lax.ppermute(field, "col", up)
    after = lax.ppermute(field, "col", down)
    groups = plane_groups()

    split = field.reshape(4, PLANE, 16, 128).transpose(1, 0, 2, 3).reshape(PLANE, 64, 128)
    got = lax.all_to_all(split, "row", 0, 0, tiled=True, axis_index_groups=groups)
    got, before, after = lax.optimization_barrier((got, before, after))
    row = lax.axis_index("row").astype(jnp.int32).reshape(1)
    mine, other = arrange(row, got)

    swap, across = z_swap(1), z_swap(-1)
    pair = lax.ppermute(other, "row", swap)
    opposite = lax.ppermute(pair, "row", across)

    second, sync2, first = factors(
        route1_cols.reshape(-1),
        route2_cols.reshape(-1),
        row,
        route1_blocks,
        route2_blocks,
    )
    ready, first = lax.optimization_barrier((mine, first))
    cross = lax.ppermute(ready, "row", across)
    turned = jnp.swapaxes(route3_factors, 1, 2)
    base = local_terms(fleet_offsets, second, turned[0], field, before, after)
    acc = near(first, turned[1], mine, pair, cross)
    acc, base, opposite = lax.optimization_barrier((acc, base, opposite))
    theirs = far(1, first, turned[1], acc, opposite)
    ours = far(0, first, turned[1], acc, opposite)
    swapped = lax.ppermute(theirs, "row", swap)

    def collect(value):
        value = value.reshape(PLANE, 64, 128)
        back = lax.all_to_all(value, "row", 0, 0, tiled=True, axis_index_groups=groups)
        return back.reshape(PLANE, 2, 4, 8, 128)

    state_out, accum_out = finish(
        poisson_weight, row, sync2, collect(ours), collect(swapped), base, accum[0]
    )
    return state_out[None], accum_out[None]


def solution(mesh):
    placed = (
        P("col", "row", None, None),
        P("col", "row", None, None),
        P(),
        P(),
        P(),
        P(),
        P(),
        P(),
        P(),
    )
    return jax.shard_map(
        local,
        mesh=mesh,
        in_specs=placed,
        out_specs=(P("col", "row", None, None), P("col", "row", None, None)),
        check_vma=False,
    )
```

```python
import functools

import jax
import jax.numpy as jnp
from jax import lax
from jax.experimental import pallas as pl
from jax.experimental.pallas import tpu as pltpu
from jax.sharding import PartitionSpec as P

NX, NZ, NY, NC = 4, 4, 4, 2
PLANE = NX * NY * NC
BF = jnp.bfloat16
F32 = jnp.float32


def row_of(x, z, y, core):
    return ((x * NZ + z % NZ) * NY + y) * NC + core


def plane_groups():
    return [
        [row_of(x, z, y, c) for x in range(NX) for y in range(NY) for c in range(NC)]
        for z in range(NZ)
    ]


def z_swap(sign):
    return [
        (row_of(x, z, y, c), row_of(x, z + (sign if (z + c) % 2 == 0 else -sign), y, c))
        for x in range(NX)
        for z in range(NZ)
        for y in range(NY)
        for c in range(NC)
    ]


def place_of(row):
    z, core = (row >> 3) & 3, row & 1
    step = 1 - 2 * ((z + core) & 1)
    return z, step, half_of(z, core)


def half_of(z, core):
    return ((z + 1 - core) >> 1) & 1


def cost(flops, moved):
    return pl.CostEstimate(flops=flops, bytes_accessed=moved, transcendentals=0)


SMALL = pltpu.CompilerParams(vmem_limit_bytes=24 * 1024 * 1024)


def iota2(shape):
    return (
        lax.broadcasted_iota(jnp.int32, shape, 0),
        lax.broadcasted_iota(jnp.int32, shape, 1),
    )


def onehot(rows_match):
    return jnp.where(rows_match, 1.0, 0.0).astype(BF)


def dot(a, b):
    return jnp.dot(a, b, preferred_element_type=F32)


def factors_kernel(cols1, cols2, row_ref, b1, b2, second, sync2, first, dense):
    second[...] = jnp.zeros_like(second)
    sync2[...] = jnp.zeros_like(sync2)
    dense[...] = jnp.zeros_like(dense)

    def place(dst, r, base, c, blk):
        zero = jnp.zeros_like(blk)
        left = jnp.concatenate([blk, zero], axis=1)
        right = jnp.concatenate([zero, blk], axis=1)
        wide = jnp.where((c & 1) == 0, left, right)
        at = (
            pl.ds(pl.multiple_of(r * 64, 64), 64),
            pl.ds(pl.multiple_of(base + (c >> 1) * 128, 128), 128),
        )
        dst[at] = dst[at] + wide

    def row(r, carry):
        for k in range(4):
            for t in range(2):
                place(dense.at[t], r, 0, cols1[t * 32 + r * 4 + k], b1[t, r, k])
            place(sync2, r, 0, cols2[32 + r * 4 + k], b2[1, r, k])
            for t, base in ((0, 0), (2, 512), (3, 1024), (4, 1536)):
                place(second, r, base, cols2[t * 32 + r * 4 + k], b2[t, r, k])
        return carry

    lax.fori_loop(0, 8, row, 0)
    me, step, _ = place_of(row_ref[0])
    i, j = iota2((512, 512))
    source = ((j >> 5) & 3) * 128 + (j >> 7) * 32 + (j & 31)
    swap = onehot(i == source)
    for d in range(2):
        at = (me + d * step) & 3
        for t in range(2):
            rows = jnp.concatenate(
                [dense[t, pl.ds(pl.multiple_of(x * 128 + at * 32, 32), 32), :] for x in range(4)],
                axis=0,
            )
            turned = dot(rows, swap).astype(BF)
            for z in range(4):
                first[d, t, ((z - me) * step) & 3] = turned[:, z * 128 : (z + 1) * 128]


def factors(cols1, cols2, row, b1, b2):
    smem = pl.BlockSpec(memory_space=pltpu.SMEM)
    vmem = pl.BlockSpec(memory_space=pltpu.VMEM)
    return pl.pallas_call(
        factors_kernel,
        out_shape=(
            jax.ShapeDtypeStruct((512, 2048), BF),
            jax.ShapeDtypeStruct((512, 512), BF),
            jax.ShapeDtypeStruct((2, 2, 4, 128, 128), BF),
        ),
        in_specs=[smem, smem, smem, vmem, vmem],
        out_specs=(vmem, vmem, vmem),
        scratch_shapes=[pltpu.VMEM((2, 512, 512), BF)],
        cost_estimate=cost(300_000_000, 8_000_000),
        compiler_params=SMALL,
        name="factors",
    )(cols1, cols2, row, b1, b2)


def arrange_kernel(row_ref, got, mine, other):
    _, _, half = place_of(row_ref[0])
    i, j = iota2((256, 256))
    move = onehot(j == ((i >> 2) & 3) * 64 + (i & 3) * 16 + (i >> 4))
    for g in range(8):
        block = got[4 * g : 4 * g + 4].reshape(256, 128)
        out = dot(move, block)
        at = slice(g * 16, g * 16 + 16)
        for m in range(8):
            low = out[m * 16 : m * 16 + 16, :]
            high = out[m * 16 + 128 : m * 16 + 144, :]
            mine[m, at, :] = jnp.where(half == 0, low, high).astype(BF)
            other[m, at, :] = jnp.where(half == 0, high, low).astype(BF)


def arrange(row, got):
    one = jax.ShapeDtypeStruct((8, 128, 128), BF)
    return pl.pallas_call(
        arrange_kernel,
        out_shape=(one, one),
        in_specs=[pl.BlockSpec(memory_space=pltpu.SMEM), pl.BlockSpec(memory_space=pltpu.VMEM)],
        cost_estimate=cost(130_000_000, 1_100_000),
        compiler_params=SMALL,
        name="arrange",
    )(row, got)


def twice(s3):
    zero = jnp.zeros_like(s3)
    return jnp.concatenate(
        [jnp.concatenate([s3, zero], axis=1), jnp.concatenate([zero, s3], axis=1)], axis=0
    )


def near_kernel(first, s3, mine, pair, cross, acc):
    s3_twice = twice(s3[...])
    for p in range(4):
        sums = [[None, None], [None, None]]
        for slot, part in ((0, mine), (1, pair), (3, cross)):
            x = jnp.concatenate([part[2 * p], part[2 * p + 1]], axis=1)
            inputs = (x, dot(x, s3_twice).astype(BF))
            for d in range(2):
                for t in range(2):
                    got = dot(first[d, t, slot], inputs[t])
                    sums[d][t] = got if sums[d][t] is None else sums[d][t] + got
        for d in range(2):
            for t in range(2):
                acc[d, t, :, p * 256 : p * 256 + 256] = sums[d][t]


def near(first, s3, mine, pair, cross):
    return pl.pallas_call(
        near_kernel,
        out_shape=jax.ShapeDtypeStruct((2, 2, 128, 1024), F32),
        cost_estimate=cost(700_000_000, 4_000_000),
        compiler_params=SMALL,
        name="near",
    )(first, s3, mine, pair, cross)


def far_kernel(d, first, s3, acc, part, out, keep):
    s3_twice = twice(s3[...])
    for p in range(4):
        at = slice(p * 256, p * 256 + 256)
        x = jnp.concatenate([part[2 * p], part[2 * p + 1]], axis=1)
        inputs = (x, dot(x, s3_twice).astype(BF))
        for t in range(2):
            keep[t, :, at] = (acc[d, t, :, at] + dot(first[d, t, 2], inputs[t])).astype(BF)
    i, j = iota2((128, 128))
    move = onehot(i == ((j >> 2) & 3) * 32 + (j & 3) * 8 + (j >> 4))
    for t in range(2):
        for g in range(8):
            rows = jnp.concatenate(
                [keep[t, g * 16 : g * 16 + 16, m * 128 : m * 128 + 128] for m in range(8)],
                axis=0,
            )
            out[4 * g : 4 * g + 4, t] = dot(move, rows).astype(BF).reshape(4, 32, 128)


def far(d, first, s3, acc, part):
    return pl.pallas_call(
        functools.partial(far_kernel, d),
        out_shape=jax.ShapeDtypeStruct((32, 2, 32, 128), BF),
        scratch_shapes=[pltpu.VMEM((2, 128, 1024), BF)],
        cost_estimate=cost(200_000_000, 2_000_000),
        compiler_params=SMALL,
        name="far",
    )(first, s3, acc, part)


def local_kernel(offsets, second, r3, state, before, after, out, stack):
    x = state[0]
    stack[0:512, :] = x
    for k in range(3):
        off = offsets[k]
        rows = slice(512 * (k + 1), 512 * (k + 2))

        @pl.when(off == 1)
        def _():
            stack[rows, :] = before[0]

        @pl.when(off == 0)
        def _():
            stack[rows, :] = state[0]

        @pl.when(off == -1)
        def _():
            stack[rows, :] = after[0]

    out[0] = x.astype(F32) + dot(x, r3[...]) + dot(second[...], stack[...])


def local_terms(offsets, second, r3, state, before, after):
    slab = pl.BlockSpec((1, 512, 128), lambda b: (b, 0, 0))
    return pl.pallas_call(
        local_kernel,
        grid=(4,),
        out_shape=jax.ShapeDtypeStruct((4, 512, 128), F32),
        in_specs=[
            pl.BlockSpec(memory_space=pltpu.SMEM),
            pl.BlockSpec((512, 2048), lambda b: (0, 0)),
            pl.BlockSpec((128, 128), lambda b: (0, 0)),
            slab,
            slab,
            slab,
        ],
        out_specs=slab,
        scratch_shapes=[pltpu.VMEM((2048, 128), BF)],
        cost_estimate=cost(1_200_000_000, 5_000_000),
        compiler_params=SMALL,
        name="local_terms",
    )(offsets, second, r3, state, before, after)


def finish_kernel(weight, row_ref, sync2, back1, back2, base, accum, state_out, accum_out):
    z, _, _ = place_of(row_ref[0])
    core = lax.broadcasted_iota(jnp.int32, (PLANE, 8, 128), 0) & 1
    low_first = jnp.where(core == 0, half_of(z, 0), half_of(z, 1)) == 0

    def joined(t):
        one, two = back1[:, t, 0].astype(F32), back2[:, t, 0].astype(F32)
        parts = [jnp.where(low_first, one, two), jnp.where(low_first, two, one)]
        return jnp.concatenate(parts, axis=1).reshape(512, 128)

    total = base[0] + joined(0) + dot(sync2[...], joined(1).astype(BF))
    state_out[0] = total.astype(BF)
    accum_out[0] = accum[0] + weight[0] * total


def finish(weight, row, sync2, back1, back2, base, accum):
    slab = pl.BlockSpec((1, 512, 128), lambda b: (b, 0, 0))
    part = pl.BlockSpec((32, 2, 1, 8, 128), lambda b: (0, 0, b, 0, 0))
    smem = pl.BlockSpec(memory_space=pltpu.SMEM)
    return pl.pallas_call(
        finish_kernel,
        grid=(4,),
        out_shape=(
            jax.ShapeDtypeStruct((4, 512, 128), BF),
            jax.ShapeDtypeStruct((4, 512, 128), F32),
        ),
        in_specs=[smem, smem, pl.BlockSpec((512, 512), lambda b: (0, 0)), part, part, slab, slab],
        out_specs=(slab, slab),
        cost_estimate=cost(300_000_000, 6_000_000),
        compiler_params=SMALL,
        name="finish",
    )(weight, row, sync2, back1, back2, base, accum)


def local(
    state,
    accum,
    poisson_weight,
    route1_blocks,
    route1_cols,
    route2_blocks,
    route2_cols,
    route3_factors,
    fleet_offsets,
):
    field = state[0]
    levels = lax.axis_size("col")
    up = [(i, i + 1) for i in range(levels - 1)]
    down = [(i + 1, i) for i in range(levels - 1)]
    before = lax.ppermute(field, "col", up)
    after = lax.ppermute(field, "col", down)
    groups = plane_groups()

    split = field.reshape(4, PLANE, 16, 128).transpose(1, 0, 2, 3).reshape(PLANE, 64, 128)
    got = lax.all_to_all(split, "row", 0, 0, tiled=True, axis_index_groups=groups)
    got, before, after = lax.optimization_barrier((got, before, after))
    row = lax.axis_index("row").astype(jnp.int32).reshape(1)
    mine, other = arrange(row, got)

    swap, across = z_swap(1), z_swap(-1)
    pair = lax.ppermute(other, "row", swap)
    opposite = lax.ppermute(pair, "row", across)

    second, sync2, first = factors(
        route1_cols.reshape(-1),
        route2_cols.reshape(-1),
        row,
        route1_blocks,
        route2_blocks,
    )
    turned = jnp.swapaxes(route3_factors, 1, 2)
    base = local_terms(fleet_offsets, second, turned[0], field, before, after)
    ready, base = lax.optimization_barrier((mine, base))
    cross = lax.ppermute(ready, "row", across)
    acc = near(first, turned[1], mine, pair, cross)
    acc, base, opposite = lax.optimization_barrier((acc, base, opposite))
    theirs = far(1, first, turned[1], acc, opposite)
    ours = far(0, first, turned[1], acc, opposite)
    swapped = lax.ppermute(theirs, "row", swap)

    def collect(value):
        value = value.reshape(PLANE, 64, 128)
        back = lax.all_to_all(value, "row", 0, 0, tiled=True, axis_index_groups=groups)
        return back.reshape(PLANE, 2, 4, 8, 128)

    state_out, accum_out = finish(
        poisson_weight, row, sync2, collect(ours), collect(swapped), base, accum[0]
    )
    return state_out[None], accum_out[None]


def solution(mesh):
    placed = (
        P("col", "row", None, None),
        P("col", "row", None, None),
        P(),
        P(),
        P(),
        P(),
        P(),
        P(),
        P(),
    )
    return jax.shard_map(
        local,
        mesh=mesh,
        in_specs=placed,
        out_specs=(P("col", "row", None, None), P("col", "row", None, None)),
        check_vma=False,
    )
```
